512 devices in a mesh: ed: 64 (over y, z), tp: 8 (over x, core).
Axes of the slice: x: 4, y: 4, z: 16, core: 2. Of those that a mesh axis runs over, the one named last changes fastest.
Arguments:
- tokens: bfloat16 [8192, 2048], P('ed'), may hold values from -6 to 6
- cotangent: bfloat16 [8192, 2048], P('ed'), may hold values from -4 to 4
- expert_ids: int32 [8192, 2], P('ed'), may hold values from 0 to 3, all different within a row; in each aligned block of 128 rows (0 to 127, 128 to 255, ...) at most 80 rows name the same one
- route_weights: float32 [8192, 2], P('ed'), may hold values from 0.1 to 0.9
- w_gate: bfloat16 [8192, 7168], P('ed', 'tp'), may hold values from -0.125 to 0.125
- w_up: bfloat16 [8192, 7168], P('ed', 'tp'), may hold values from -0.125 to 0.125
- w_down: bfloat16 [7168, 8192], P('tp', 'ed'), may hold values from -0.0625 to 0.0625
Outputs:
- mixed: bfloat16 [8192, 2048], P('ed', 'tp')
- grad_tokens: bfloat16 [8192, 2048], P('ed', 'tp')
The draws below stay inside these ranges and needn't reach their ends.
Inputs may be any that keep to these rules, and one draw needn't show every extreme that they name: `expert_ids`: the two experts of a token differ. Among the 128 tokens of one index of ed (aligned blocks), each expert is named by at most 80 tokens, and in some blocks one expert by exactly 80.
All inputs are finite; a program needn't handle non-finite values.
Results may differ from the reference program's by a relative error of at most 0.015.
Values may be sent and summed in bfloat16 or wider, within the bound.
A program may use at most 128 MiB of HBM per device.

```python
import math
import jax
import jax.numpy as jnp
import numpy as np
from jax import lax

D = 2048
FF = 7168
EXPERTS = 4
TOP = 2
TOK_DEV = 128
CAP = 80
TOKENS = 8192
N_ED = 64
N_TP = 8


def level_of(rng, shape, split, smallest, high):
    gain, own = 1.0, jax.random.fold_in(rng, 6)
    for position, parts in split:
        steps = jnp.exp(jax.random.uniform(jax.random.fold_in(own, position), (parts,), jnp.float32, smallest / len(split), high / len(split)))
        gain = gain * jnp.repeat(steps, shape[position] // parts).reshape([-1 if axis == position else 1 for axis in range(len(shape))])
    return gain


def shared_out(stream_key, own, number, rows, amount, top, most, slope):
    sequence = jax.random.permutation(stream_key, amount)
    packed, common = shares(amount, rows * top, most, slope, True), shares(amount, rows * top, most, slope, False)
    places = jnp.arange(amount)

    def named(lengths, offset_by):
        used = int((lengths > 0).sum())
        fixed = max(1, used // 4)
        moved = fixed + (places - fixed + offset_by * (used - fixed)) % max(1, amount - fixed)
        return jnp.zeros((amount,), jnp.int32).at[sequence[jnp.where(places < fixed, places, moved)]].set(jnp.asarray(lengths, jnp.int32))

    lengths = jnp.where(number % 4 == 0, named(packed, number // 4), named(common, number - number // 4 - 1))
    mixed = jax.random.permutation(jax.random.fold_in(own, 3), amount)
    donor, taker = mixed[0:amount // 2 * 2:2], mixed[1:amount // 2 * 2:2]
    margin = jnp.minimum(lengths[donor] - 1, most - lengths[taker]) // 2
    margin = jnp.where((donor == sequence[0]) | (taker == sequence[0]) | (lengths[taker] == 0), 0, jnp.maximum(margin, 0))
    moved = jax.random.randint(jax.random.fold_in(own, 4), (amount // 2,), 0, 1 << 20) % (margin + 1)
    lengths = lengths.at[donor].add(-moved).at[taker].add(moved)
    members = jnp.searchsorted(jnp.cumsum(lengths), jnp.arange(rows * top), side="right").astype(jnp.int32)
    listing = members.reshape(top, rows).T
    listing = listing[jax.random.permutation(jax.random.fold_in(own, 1), rows)]
    offset_by = jax.random.randint(jax.random.fold_in(own, 2), (rows, 1), 0, top)
    return jnp.take_along_axis(listing, (jnp.arange(top)[None, :] + offset_by) % top, axis=1)


def shares(count, total, reach, lean, full):
    portions = [(1 << 20) // math.isqrt(standing ** lean) + 1 for standing in range(1, count + 1)]
    largest = reach if full else min(reach, max(-(-total // count), total * portions[0] // sum(portions)))
    least = 1 if total - largest >= count - 1 else 0
    holding, rest = [largest] + [least] * (count - 1), total - largest - least * (count - 1)
    while rest > 0:
        candidates = [i for i in range(1, count) if holding[i] < largest] or [i for i in range(1, count) if holding[i] < reach]
        whole, left = sum([portions[i] for i in candidates]), rest
        for i in candidates:
            extra = min(reach - holding[i], max(1, left * portions[i] // whole), rest)
            holding[i] = holding[i] + extra
            rest = rest - extra
    return np.array(holding)


def normal_values(key, extent, scale, reach, cuts=(), kind=jnp.bfloat16):
    level = level_of(key, extent, cuts, -0.22, 0.18) if cuts else 1.0
    values = jax.random.normal(key, extent, jnp.float32) * scale * level
    return jnp.minimum(jnp.maximum(values, -reach), reach).astype(kind)


def setup_inputs(seed: int = 0) -> dict:
    key_list = jax.random.split(jax.random.key(seed), 8)
    tokens = normal_values(key_list[0], (TOKENS, D), 1.0, 6.0, ((0, 64),))
    cotangent = normal_values(key_list[1], (TOKENS, D), 0.5, 4.0, ((0, 64),))
    expert_ids_keys = jax.random.split(jax.random.fold_in(key_list[2], 1), TOKENS // TOK_DEV)
    expert_ids_turns = jax.random.permutation(jax.random.fold_in(key_list[2], 3), TOKENS // TOK_DEV)
    expert_ids = jax.vmap(lambda own, number: shared_out(jax.random.fold_in(key_list[2], 2), own, number, TOK_DEV, EXPERTS, TOP, CAP, 2))(expert_ids_keys, expert_ids_turns).reshape((TOKENS, TOP))
    route_weights = jnp.clip(0.1 + 0.79999997 * jax.random.uniform(key_list[3], (TOKENS, TOP), jnp.float32) ** level_of(key_list[3], (TOKENS, TOP), ((0, 64),), -0.2, 0.2), 0.1, 0.9)
    w_gate = normal_values(key_list[4], (EXPERTS * D, FF), D ** -0.5, 0.125, ((0, 64), (1, 8)))
    w_up = normal_values(key_list[5], (EXPERTS * D, FF), D ** -0.5, 0.125, ((0, 64), (1, 8)))
    w_down = normal_values(key_list[6], (FF, EXPERTS * D), FF ** -0.5, 0.0625, ((0, 8), (1, 64)))
    return {"tokens": tokens, "cotangent": cotangent, "expert_ids": expert_ids, "route_weights": route_weights, "w_gate": w_gate, "w_up": w_up, "w_down": w_down}


def activate(gate_pre, up_pre, hidden_grad):
    sig_gate = jax.nn.sigmoid(gate_pre)
    silu_gate = gate_pre * sig_gate
    hidden = (silu_gate * up_pre).astype(jnp.bfloat16)
    gate_grad = (hidden_grad * up_pre * sig_gate * (1.0 + gate_pre * (1.0 - sig_gate))).astype(jnp.bfloat16)
    up_grad = (hidden_grad * silu_gate).astype(jnp.bfloat16)
    return hidden, gate_grad, up_grad


def sliced_sums(hidden, gate_grad, up_grad, expert_gate, expert_up, expert_down):
    slice_width = FF // N_TP
    out_total = jnp.zeros((hidden.shape[0], D), jnp.float32)
    in_total = jnp.zeros((hidden.shape[0], D), jnp.float32)
    for part in range(N_TP):
        lower = part * slice_width
        upper = lower + slice_width
        out_piece = jnp.dot(hidden[:, lower:upper], expert_down[lower:upper], preferred_element_type=jnp.float32).astype(jnp.bfloat16)
        in_piece = jnp.dot(gate_grad[:, lower:upper], expert_gate[:, lower:upper].T, preferred_element_type=jnp.float32)
        in_piece = (in_piece + jnp.dot(up_grad[:, lower:upper], expert_up[:, lower:upper].T, preferred_element_type=jnp.float32)).astype(jnp.bfloat16)
        out_piece, in_piece = lax.optimization_barrier((out_piece, in_piece))
        out_total = out_total + out_piece.astype(jnp.float32)
        in_total = in_total + in_piece.astype(jnp.float32)
    return out_total.astype(jnp.bfloat16), in_total.astype(jnp.bfloat16)


def reference(tokens, cotangent, expert_ids, route_weights, w_gate, w_up, w_down):
    routes = expert_ids.reshape(-1).astype(jnp.int32)
    route_token = (jnp.arange(TOKENS * TOP, dtype=jnp.int32) // TOP).astype(jnp.int32)
    flat_weights = route_weights.reshape(-1).astype(jnp.float32)
    slot_total = N_ED * CAP

    def one_expert(expert):
        order_key = (routes != expert).astype(jnp.int32)
        ordering = jnp.argsort(order_key, stable=True)[:slot_total].astype(jnp.int32)
        valid_rows = routes[ordering] == expert
        row_tokens = route_token[ordering]
        rows_in = tokens[row_tokens]
        weight_rows = jnp.where(valid_rows, flat_weights[ordering], jnp.float32(0.0))
        start = (expert * D).astype(jnp.int32)
        expert_gate = lax.dynamic_slice_in_dim(w_gate, start, D, 0)
        expert_up = lax.dynamic_slice_in_dim(w_up, start, D, 0)
        expert_down = lax.dynamic_slice_in_dim(w_down, start, D, 1)
        gate_pre = jnp.dot(rows_in, expert_gate, preferred_element_type=jnp.float32)
        up_pre = jnp.dot(rows_in, expert_up, preferred_element_type=jnp.float32)
        route_cot = (weight_rows[:, None] * cotangent[row_tokens].astype(jnp.float32)).astype(jnp.bfloat16)
        hidden_grad = jnp.dot(route_cot, expert_down.T, preferred_element_type=jnp.float32)
        hidden, gate_grad, up_grad = activate(gate_pre, up_pre, hidden_grad)
        route_out, route_in = sliced_sums(hidden, gate_grad, up_grad, expert_gate, expert_up, expert_down)
        valid_float = valid_rows.astype(jnp.float32)[:, None]
        out_sum = jnp.zeros((TOKENS, D), jnp.float32).at[row_tokens].add(weight_rows[:, None] * route_out.astype(jnp.float32))
        in_sum = jnp.zeros((TOKENS, D), jnp.float32).at[row_tokens].add(valid_float * route_in.astype(jnp.float32))
        return out_sum, in_sum

    out_all, in_all = lax.map(one_expert, jnp.arange(EXPERTS, dtype=jnp.int32))
    mixed = jnp.sum(out_all, axis=0).astype(jnp.bfloat16)
    grad_tokens = jnp.sum(in_all, axis=0).astype(jnp.bfloat16)
    return mixed, grad_tokens
```

```python
import jax
import jax.numpy as jnp
import numpy as np
from jax import lax
from jax.sharding import Mesh
from jax.sharding import PartitionSpec as P

EXPERTS = 4
TOP = 2
CAP = 80


def activate(gate_pre, up_pre, hidden_grad):
    sig_gate = jax.nn.sigmoid(gate_pre)
    silu_gate = gate_pre * sig_gate
    hidden = (silu_gate * up_pre).astype(jnp.bfloat16)
    gate_grad = (hidden_grad * up_pre * sig_gate * (1.0 + gate_pre * (1.0 - sig_gate))).astype(
        jnp.bfloat16
    )
    up_grad = (hidden_grad * silu_gate).astype(jnp.bfloat16)
    return (hidden, gate_grad, up_grad)


def per_device(tokens, cotangent, expert_ids, route_weights, w_gate, w_up, w_down):
    plane_count = lax.axis_size("ey")
    slot_count = EXPERTS * CAP
    tok_count = tokens.shape[0]
    model_width = tokens.shape[1]
    routes = expert_ids.reshape(-1)
    onehot = (routes[:, None] == jnp.arange(EXPERTS, dtype=jnp.int32)[None, :]).astype(jnp.int32)
    before = jnp.cumsum(onehot, axis=0) - onehot
    slot_place = jnp.sum(before * onehot, axis=1)
    target = routes * CAP + slot_place
    matches = (jnp.arange(slot_count, dtype=jnp.int32)[:, None] == target[None, :]).reshape(
        slot_count, tok_count, TOP
    )
    picker = jnp.any(matches, axis=2)
    slot_weight = jnp.sum(
        jnp.where(matches, route_weights[None, :, :], jnp.float32(0.0)), axis=(1, 2)
    )
    picker_low = picker.astype(jnp.bfloat16)
    sent_tokens = jnp.dot(picker_low, tokens, preferred_element_type=jnp.float32)
    sent_tokens = sent_tokens.astype(jnp.bfloat16).reshape(plane_count, CAP, model_width)
    sent_cot = jnp.dot(picker_low, cotangent, preferred_element_type=jnp.float32)
    sent_cot = (
        (sent_cot * slot_weight[:, None]).astype(jnp.bfloat16).reshape(plane_count, CAP, model_width)
    )
    gate_full = lax.all_gather(w_gate, "ez", axis=0, tiled=True)
    up_full = lax.all_gather(w_up, "ez", axis=0, tiled=True)
    down_pieces = lax.all_gather(w_down, "ez", axis=0, tiled=False)
    member_tokens = lax.all_to_all(sent_tokens, "ey", split_axis=0, concat_axis=0, tiled=True)
    member_cot = lax.all_to_all(sent_cot, "ey", split_axis=0, concat_axis=0, tiled=True)
    row_total = plane_count * CAP
    member_count = down_pieces.shape[0]
    block_width = down_pieces.shape[2]
    member_tokens = member_tokens.reshape(row_total, model_width)
    member_cot = member_cot.reshape(row_total, member_count, block_width)
    gate_pre = jnp.dot(member_tokens, gate_full, preferred_element_type=jnp.float32)
    up_pre = jnp.dot(member_tokens, up_full, preferred_element_type=jnp.float32)
    hidden_grad = lax.dot_general(
        member_cot, down_pieces, (((1, 2), (0, 2)), ((), ())), preferred_element_type=jnp.float32
    )
    hidden, gate_grad, up_grad = activate(gate_pre, up_pre, hidden_grad)
    out_part = lax.dot_general(
        hidden, down_pieces, (((1,), (1,)), ((), ())), preferred_element_type=jnp.float32
    )
    out_part = out_part.reshape(row_total, model_width)
    in_part = lax.dot_general(
        gate_grad, gate_full, (((1,), (1,)), ((), ())), preferred_element_type=jnp.float32
    )
    in_part = in_part + lax.dot_general(
        up_grad, up_full, (((1,), (1,)), ((), ())), preferred_element_type=jnp.float32
    )
    results = jnp.stack([out_part, in_part], axis=1)
    summed = lax.psum_scatter(results.astype(jnp.bfloat16), "tp", scatter_dimension=2, tiled=True)
    rounded = summed.reshape(plane_count, CAP, 2, -1)
    returned = lax.all_to_all(rounded, "ey", split_axis=0, concat_axis=0, tiled=True)
    returned = returned.reshape(slot_count, 2, -1).astype(jnp.float32)
    picker_full = picker.astype(jnp.float32)
    weighted = picker_full * slot_weight[:, None]
    mixed = jnp.dot(weighted.T, returned[:, 0], precision=lax.Precision.HIGHEST).astype(
        jnp.bfloat16
    )
    grad_tokens = jnp.dot(picker_full.T, returned[:, 1], precision=lax.Precision.HIGHEST).astype(
        jnp.bfloat16
    )
    return (mixed, grad_tokens)


def solution(mesh):
    ed_size = mesh.shape["ed"]
    member_count = ed_size // EXPERTS
    devices = np.asarray(mesh.devices).reshape(EXPERTS, member_count, mesh.shape["tp"])
    split_mesh = Mesh(devices, ("ey", "ez", "tp"))
    ed = ("ey", "ez")
    return jax.shard_map(
        per_device,
        mesh=split_mesh,
        in_specs=(
            P(ed, None),
            P(ed, None),
            P(ed, None),
            P(ed, None),
            P(ed, "tp"),
            P(ed, "tp"),
            P("tp", ed),
        ),
        out_specs=(P(ed, "tp"), P(ed, "tp")),
        check_vma=False,
    )
```

```python
import jax
import jax.numpy as jnp
import numpy as np
from jax import lax
from jax.sharding import Mesh
from jax.sharding import PartitionSpec as P

EXPERTS = 4
TOP = 2
CAP = 80


def activate(gate_pre, up_pre, hidden_grad):
    sig_gate = jax.nn.sigmoid(gate_pre)
    silu_gate = gate_pre * sig_gate
    hidden = (silu_gate * up_pre).astype(jnp.bfloat16)
    gate_grad = (hidden_grad * up_pre * sig_gate * (1.0 + gate_pre * (1.0 - sig_gate))).astype(
        jnp.bfloat16
    )
    up_grad = (hidden_grad * silu_gate).astype(jnp.bfloat16)
    return (hidden, gate_grad, up_grad)


def per_device(tokens, cotangent, expert_ids, route_weights, w_gate, w_up, w_down):
    plane_count = lax.axis_size("ey")
    slot_count = EXPERTS * CAP
    tok_count = tokens.shape[0]
    model_width = tokens.shape[1]
    routes = expert_ids.reshape(-1)
    onehot = (routes[:, None] == jnp.arange(EXPERTS, dtype=jnp.int32)[None, :]).astype(jnp.int32)
    before = jnp.cumsum(onehot, axis=0) - onehot
    slot_place = jnp.sum(before * onehot, axis=1)
    target = routes * CAP + slot_place
    matches = (jnp.arange(slot_count, dtype=jnp.int32)[:, None] == target[None, :]).reshape(
        slot_count, tok_count, TOP
    )
    picker = jnp.any(matches, axis=2)
    slot_weight = jnp.sum(
        jnp.where(matches, route_weights[None, :, :], jnp.float32(0.0)), axis=(1, 2)
    )
    picker_low = picker.astype(jnp.bfloat16)
    sent_tokens = jnp.dot(picker_low, tokens, preferred_element_type=jnp.float32)
    sent_tokens = sent_tokens.astype(jnp.bfloat16).reshape(plane_count, CAP, model_width)
    sent_cot = jnp.dot(picker_low, cotangent, preferred_element_type=jnp.float32)
    sent_cot = (
        (sent_cot * slot_weight[:, None]).astype(jnp.bfloat16).reshape(plane_count, CAP, model_width)
    )
    member_count = lax.axis_size("ez")
    place = lax.axis_index("ez")
    block_width = w_gate.shape[0]
    stacked = jnp.stack([w_gate, w_up, w_down.T], axis=0)
    forward = [(i, (i + 1) % member_count) for i in range(member_count)]
    backward = [(i, (i - 1) % member_count) for i in range(member_count)]
    half_steps = member_count // 2
    cw = stacked
    ccw = stacked
    by_distance = [None] * member_count
    by_distance[0] = stacked
    for step in range(1, half_steps):
        cw = lax.ppermute(cw, "ez", forward)
        ccw = lax.ppermute(ccw, "ez", backward)
        by_distance[step] = cw
        by_distance[member_count - step] = ccw
    cut = block_width // 2
    far_low = lax.ppermute(cw[:, :cut], "ez", forward)
    far_high = lax.ppermute(ccw[:, cut:], "ez", backward)
    by_distance[half_steps] = jnp.concatenate([far_low, far_high], axis=1)
    gathered = jnp.stack(by_distance, axis=0)
    origin = (place - jnp.arange(member_count, dtype=jnp.int32)) % member_count
    gathered = jnp.take(gathered, origin, axis=0)
    gate_full = gathered[:, 0].reshape(member_count * block_width, -1)
    up_full = gathered[:, 1].reshape(member_count * block_width, -1)
    down_full = gathered[:, 2].reshape(member_count * block_width, -1)
    member_tokens = lax.all_to_all(sent_tokens, "ey", split_axis=0, concat_axis=0, tiled=True)
    member_cot = lax.all_to_all(sent_cot, "ey", split_axis=0, concat_axis=0, tiled=True)
    row_total = plane_count * CAP
    member_tokens = member_tokens.reshape(row_total, model_width)
    member_cot = member_cot.reshape(row_total, model_width)
    gate_pre = jnp.dot(member_tokens, gate_full, preferred_element_type=jnp.float32)
    up_pre = jnp.dot(member_tokens, up_full, preferred_element_type=jnp.float32)
    hidden_grad = jnp.dot(member_cot, down_full, preferred_element_type=jnp.float32)
    hidden, gate_grad, up_grad = activate(gate_pre, up_pre, hidden_grad)
    out_part = lax.dot_general(
        hidden, down_full, (((1,), (1,)), ((), ())), preferred_element_type=jnp.float32
    )
    in_part = lax.dot_general(
        gate_grad, gate_full, (((1,), (1,)), ((), ())), preferred_element_type=jnp.float32
    )
    in_part = in_part + lax.dot_general(
        up_grad, up_full, (((1,), (1,)), ((), ())), preferred_element_type=jnp.float32
    )
    results = jnp.stack([out_part, in_part], axis=1)
    summed = lax.psum_scatter(results.astype(jnp.bfloat16), "tp", scatter_dimension=2, tiled=True)
    rounded = summed.reshape(plane_count, CAP, 2, -1)
    returned = lax.all_to_all(rounded, "ey", split_axis=0, concat_axis=0, tiled=True)
    returned = returned.reshape(slot_count, 2, -1).astype(jnp.float32)
    picker_full = picker.astype(jnp.float32)
    weighted = picker_full * slot_weight[:, None]
    mixed = jnp.dot(weighted.T, returned[:, 0], precision=lax.Precision.HIGHEST).astype(
        jnp.bfloat16
    )
    grad_tokens = jnp.dot(picker_full.T, returned[:, 1], precision=lax.Precision.HIGHEST).astype(
        jnp.bfloat16
    )
    return (mixed, grad_tokens)


def solution(mesh):
    ed_size = mesh.shape["ed"]
    member_count = ed_size // EXPERTS
    devices = np.asarray(mesh.devices).reshape(EXPERTS, member_count, mesh.shape["tp"])
    split_mesh = Mesh(devices, ("ey", "ez", "tp"))
    ed = ("ey", "ez")
    return jax.shard_map(
        per_device,
        mesh=split_mesh,
        in_specs=(
            P(ed, None),
            P(ed, None),
            P(ed, None),
            P(ed, None),
            P(ed, "tp"),
            P(ed, "tp"),
            P("tp", ed),
        ),
        out_specs=(P(ed, "tp"), P(ed, "tp")),
        check_vma=False,
    )
```

```python
import jax
import jax.numpy as jnp
import numpy as np
from jax import lax
from jax.sharding import Mesh
from jax.sharding import PartitionSpec as P

EXPERTS = 4
TOP = 2
CAP = 80


def activate(gate_pre, up_pre, hidden_grad):
    sig_gate = jax.nn.sigmoid(gate_pre)
    silu_gate = gate_pre * sig_gate
    hidden = (silu_gate * up_pre).astype(jnp.bfloat16)
    gate_grad = (hidden_grad * up_pre * sig_gate * (1.0 + gate_pre * (1.0 - sig_gate))).astype(
        jnp.bfloat16
    )
    up_grad = (hidden_grad * silu_gate).astype(jnp.bfloat16)
    return (hidden, gate_grad, up_grad)


def per_device(tokens, cotangent, expert_ids, route_weights, w_gate, w_up, w_down):
    plane_count = lax.axis_size("ey")
    slot_count = EXPERTS * CAP
    tok_count = tokens.shape[0]
    model_width = tokens.shape[1]
    routes = expert_ids.reshape(-1)
    onehot = (routes[:, None] == jnp.arange(EXPERTS, dtype=jnp.int32)[None, :]).astype(jnp.int32)
    before = jnp.cumsum(onehot, axis=0) - onehot
    slot_place = jnp.sum(before * onehot, axis=1)
    target = routes * CAP + slot_place
    matches = (jnp.arange(slot_count, dtype=jnp.int32)[:, None] == target[None, :]).reshape(
        slot_count, tok_count, TOP
    )
    picker = jnp.any(matches, axis=2)
    slot_weight = jnp.sum(
        jnp.where(matches, route_weights[None, :, :], jnp.float32(0.0)), axis=(1, 2)
    )
    picker_low = picker.astype(jnp.bfloat16)
    sent_tokens = jnp.dot(picker_low, tokens, preferred_element_type=jnp.float32)
    sent_tokens = sent_tokens.astype(jnp.bfloat16).reshape(plane_count, CAP, model_width)
    sent_cot = jnp.dot(picker_low, cotangent, preferred_element_type=jnp.float32)
    sent_cot = (
        (sent_cot * slot_weight[:, None]).astype(jnp.bfloat16).reshape(plane_count, CAP, model_width)
    )
    member_count = lax.axis_size("ez")
    place = lax.axis_index("ez")
    block_width = w_gate.shape[0]
    stacked = jnp.stack([w_gate, w_up, w_down.T], axis=0)
    forward = [(i, (i + 1) % member_count) for i in range(member_count)]
    backward = [(i, (i - 1) % member_count) for i in range(member_count)]
    half_steps = member_count // 2
    cw = stacked
    ccw = stacked
    by_distance = [None] * member_count
    by_distance[0] = stacked
    for step in range(1, half_steps):
        cw = lax.ppermute(cw, "ez", forward)
        ccw = lax.ppermute(ccw, "ez", backward)
        by_distance[step] = cw
        by_distance[member_count - step] = ccw
    cut = block_width // 2
    far_low = lax.ppermute(cw[:, :cut], "ez", forward)
    far_high = lax.ppermute(ccw[:, cut:], "ez", backward)
    by_distance[half_steps] = jnp.concatenate([far_low, far_high], axis=1)
    origin = (place - jnp.arange(member_count, dtype=jnp.int32)) % member_count
    gate_full = jnp.concatenate([chunk[0] for chunk in by_distance], axis=0)
    up_full = jnp.concatenate([chunk[1] for chunk in by_distance], axis=0)
    down_full = jnp.concatenate([chunk[2] for chunk in by_distance], axis=0)
    member_tokens = lax.all_to_all(sent_tokens, "ey", split_axis=0, concat_axis=0, tiled=True)
    member_cot = lax.all_to_all(sent_cot, "ey", split_axis=0, concat_axis=0, tiled=True)
    row_total = plane_count * CAP
    member_tokens = jnp.take(
        member_tokens.reshape(row_total, member_count, block_width), origin, axis=1
    ).reshape(row_total, model_width)
    member_cot = jnp.take(
        member_cot.reshape(row_total, member_count, block_width), origin, axis=1
    ).reshape(row_total, model_width)
    gate_pre = jnp.dot(member_tokens, gate_full, preferred_element_type=jnp.float32)
    up_pre = jnp.dot(member_tokens, up_full, preferred_element_type=jnp.float32)
    hidden_grad = jnp.dot(member_cot, down_full, preferred_element_type=jnp.float32)
    hidden, gate_grad, up_grad = activate(gate_pre, up_pre, hidden_grad)
    out_part = lax.dot_general(
        hidden, down_full, (((1,), (1,)), ((), ())), preferred_element_type=jnp.float32
    )
    in_part = lax.dot_general(
        gate_grad, gate_full, (((1,), (1,)), ((), ())), preferred_element_type=jnp.float32
    )
    in_part = in_part + lax.dot_general(
        up_grad, up_full, (((1,), (1,)), ((), ())), preferred_element_type=jnp.float32
    )
    results = jnp.stack([out_part, in_part], axis=1).astype(jnp.bfloat16)
    results = jnp.take(
        results.reshape(row_total, 2, member_count, block_width), origin, axis=2
    ).reshape(row_total, 2, model_width)
    summed = lax.psum_scatter(results, "tp", scatter_dimension=2, tiled=True)
    rounded = summed.reshape(plane_count, CAP, 2, -1)
    returned = lax.all_to_all(rounded, "ey", split_axis=0, concat_axis=0, tiled=True)
    returned = returned.reshape(slot_count, 2, -1).astype(jnp.float32)
    picker_full = picker.astype(jnp.float32)
    weighted = picker_full * slot_weight[:, None]
    mixed = jnp.dot(weighted.T, returned[:, 0], precision=lax.Precision.HIGHEST).astype(
        jnp.bfloat16
    )
    grad_tokens = jnp.dot(picker_full.T, returned[:, 1], precision=lax.Precision.HIGHEST).astype(
        jnp.bfloat16
    )
    return (mixed, grad_tokens)


def solution(mesh):
    ed_size = mesh.shape["ed"]
    member_count = ed_size // EXPERTS
    devices = np.asarray(mesh.devices).reshape(EXPERTS, member_count, mesh.shape["tp"])
    split_mesh = Mesh(devices, ("ey", "ez", "tp"))
    ed = ("ey", "ez")
    return jax.shard_map(
        per_device,
        mesh=split_mesh,
        in_specs=(
            P(ed, None),
            P(ed, None),
            P(ed, None),
            P(ed, None),
            P(ed, "tp"),
            P(ed, "tp"),
            P("tp", ed),
        ),
        out_specs=(P(ed, "tp"), P(ed, "tp")),
        check_vma=False,
    )
```

```python
import jax
import jax.numpy as jnp
import numpy as np
from jax import lax
from jax.sharding import Mesh
from jax.sharding import PartitionSpec as P

EXPERTS = 4
TOP = 2
CAP = 80


def activate(gate_pre, up_pre, hidden_grad):
    sig_gate = jax.nn.sigmoid(gate_pre)
    silu_gate = gate_pre * sig_gate
    hidden = (silu_gate * up_pre).astype(jnp.bfloat16)
    gate_grad = (hidden_grad * up_pre * sig_gate * (1.0 + gate_pre * (1.0 - sig_gate))).astype(
        jnp.bfloat16
    )
    up_grad = (hidden_grad * silu_gate).astype(jnp.bfloat16)
    return (hidden, gate_grad, up_grad)


def per_device(tokens, cotangent, expert_ids, route_weights, w_gate, w_up, w_down):
    plane_count = lax.axis_size("ey")
    slot_count = EXPERTS * CAP
    tok_count = tokens.shape[0]
    model_width = tokens.shape[1]
    routes = expert_ids.reshape(-1)
    onehot = (routes[:, None] == jnp.arange(EXPERTS, dtype=jnp.int32)[None, :]).astype(jnp.int32)
    before = jnp.cumsum(onehot, axis=0) - onehot
    slot_place = jnp.sum(before * onehot, axis=1)
    target = routes * CAP + slot_place
    matches = (jnp.arange(slot_count, dtype=jnp.int32)[:, None] == target[None, :]).reshape(
        slot_count, tok_count, TOP
    )
    picker = jnp.any(matches, axis=2)
    slot_weight = jnp.sum(
        jnp.where(matches, route_weights[None, :, :], jnp.float32(0.0)), axis=(1, 2)
    )
    picker_low = picker.astype(jnp.bfloat16)
    sent_tokens = jnp.dot(picker_low, tokens, preferred_element_type=jnp.float32)
    sent_tokens = sent_tokens.astype(jnp.bfloat16).reshape(plane_count, CAP, model_width)
    sent_cot = jnp.dot(picker_low, cotangent, preferred_element_type=jnp.float32)
    sent_cot = (
        (sent_cot * slot_weight[:, None]).astype(jnp.bfloat16).reshape(plane_count, CAP, model_width)
    )
    member_count = lax.axis_size("ez")
    place = lax.axis_index("ez")
    block_width = w_gate.shape[0]
    stacked = jnp.stack([w_gate, w_up, w_down.T], axis=0)
    forward = [(i, (i + 1) % member_count) for i in range(member_count)]
    backward = [(i, (i - 1) % member_count) for i in range(member_count)]
    half_steps = member_count // 2
    cw = stacked
    ccw = stacked
    by_distance = [None] * member_count
    by_distance[0] = stacked
    for step in range(1, half_steps):
        cw = lax.ppermute(cw, "ez", forward)
        ccw = lax.ppermute(ccw, "ez", backward)
        by_distance[step] = cw
        by_distance[member_count - step] = ccw
    cut = block_width // 2
    far_low = lax.ppermute(cw[:, :cut], "ez", forward)
    far_high = lax.ppermute(ccw[:, cut:], "ez", backward)
    by_distance[half_steps] = jnp.concatenate([far_low, far_high], axis=1)
    order = [0]
    for step in range(1, half_steps):
        order += [step, member_count - step]
    order += [half_steps]
    early = 1 + 2 * (half_steps // 2)
    group_a, group_b = order[:early], order[early:]
    origin = (place - jnp.asarray(order, dtype=jnp.int32)) % member_count
    back_index = jnp.asarray(np.argsort(order), dtype=jnp.int32)
    back = jnp.take(back_index, (place - jnp.arange(member_count, dtype=jnp.int32)) % member_count)

    def joined(group, which):
        return jnp.concatenate([by_distance[k][which] for k in group], axis=0)

    gate_a, gate_b = joined(group_a, 0), joined(group_b, 0)
    up_a, up_b = joined(group_a, 1), joined(group_b, 1)
    down_a, down_b = joined(group_a, 2), joined(group_b, 2)
    cut_at = early * block_width
    member_tokens = lax.all_to_all(sent_tokens, "ey", split_axis=0, concat_axis=0, tiled=True)
    member_cot = lax.all_to_all(sent_cot, "ey", split_axis=0, concat_axis=0, tiled=True)
    row_total = plane_count * CAP
    member_tokens = jnp.take(
        member_tokens.reshape(row_total, member_count, block_width), origin, axis=1
    ).reshape(row_total, model_width)
    member_cot = jnp.take(
        member_cot.reshape(row_total, member_count, block_width), origin, axis=1
    ).reshape(row_total, model_width)
    tokens_a, tokens_b = member_tokens[:, :cut_at], member_tokens[:, cut_at:]
    cot_a, cot_b = member_cot[:, :cut_at], member_cot[:, cut_at:]

    def dot(left, right):
        return jnp.dot(left, right, preferred_element_type=jnp.float32)

    def dot_t(left, right):
        return lax.dot_general(
            left, right, (((1,), (1,)), ((), ())), preferred_element_type=jnp.float32
        )

    gate_pre = dot(tokens_a, gate_a) + dot(tokens_b, gate_b)
    up_pre = dot(tokens_a, up_a) + dot(tokens_b, up_b)
    hidden_grad = dot(cot_a, down_a) + dot(cot_b, down_b)
    hidden, gate_grad, up_grad = activate(gate_pre, up_pre, hidden_grad)
    out_part = jnp.concatenate([dot_t(hidden, down_a), dot_t(hidden, down_b)], axis=1)
    in_part = jnp.concatenate(
        [
            dot_t(gate_grad, gate_a) + dot_t(up_grad, up_a),
            dot_t(gate_grad, gate_b) + dot_t(up_grad, up_b),
        ],
        axis=1,
    )
    results = jnp.stack([out_part, in_part], axis=1).astype(jnp.bfloat16)
    results = jnp.take(
        results.reshape(row_total, 2, member_count, block_width), back, axis=2
    )
    pair_count = lax.axis_size("tc")
    core = lax.axis_index("tc")
    out_width = model_width // (lax.axis_size("tx") * pair_count)
    results = results.reshape(row_total, 2, -1, pair_count, out_width)
    own = jnp.where(core == 0, results[:, :, :, 0], results[:, :, :, 1])
    other = jnp.where(core == 0, results[:, :, :, 1], results[:, :, :, 0])
    other = lax.ppermute(other, "tc", [(0, 1), (1, 0)])
    pair_sum = (own.astype(jnp.float32) + other.astype(jnp.float32)).astype(jnp.bfloat16)
    summed = lax.psum_scatter(pair_sum, "tx", scatter_dimension=2, tiled=True)
    rounded = summed.reshape(plane_count, CAP, 2, -1)
    returned = lax.all_to_all(rounded, "ey", split_axis=0, concat_axis=0, tiled=True)
    returned = returned.reshape(slot_count, 2, -1).astype(jnp.float32)
    picker_full = picker.astype(jnp.float32)
    weighted = picker_full * slot_weight[:, None]
    mixed = jnp.dot(weighted.T, returned[:, 0], precision=lax.Precision.HIGHEST).astype(
        jnp.bfloat16
    )
    grad_tokens = jnp.dot(picker_full.T, returned[:, 1], precision=lax.Precision.HIGHEST).astype(
        jnp.bfloat16
    )
    return (mixed, grad_tokens)


def solution(mesh):
    ed_size = mesh.shape["ed"]
    member_count = ed_size // EXPERTS
    pair_count = 2
    devices = np.asarray(mesh.devices).reshape(
        EXPERTS, member_count, mesh.shape["tp"] // pair_count, pair_count
    )
    split_mesh = Mesh(devices, ("ey", "ez", "tx", "tc"))
    ed = ("ey", "ez")
    tp = ("tx", "tc")
    return jax.shard_map(
        per_device,
        mesh=split_mesh,
        in_specs=(
            P(ed, None),
            P(ed, None),
            P(ed, None),
            P(ed, None),
            P(ed, tp),
            P(ed, tp),
            P(tp, ed),
        ),
        out_specs=(P(ed, tp), P(ed, tp)),
        check_vma=False,
    )
```

```python
import jax
import jax.numpy as jnp
import numpy as np
from jax import lax
from jax.sharding import Mesh
from jax.sharding import PartitionSpec as P

EXPERTS = 4
TOP = 2
CAP = 80


def activate(gate_pre, up_pre, hidden_grad):
    sig_gate = jax.nn.sigmoid(gate_pre)
    silu_gate = gate_pre * sig_gate
    hidden = (silu_gate * up_pre).astype(jnp.bfloat16)
    gate_grad = (hidden_grad * up_pre * sig_gate * (1.0 + gate_pre * (1.0 - sig_gate))).astype(
        jnp.bfloat16
    )
    up_grad = (hidden_grad * silu_gate).astype(jnp.bfloat16)
    return (hidden, gate_grad, up_grad)


def per_device(tokens, cotangent, expert_ids, route_weights, w_gate, w_up, w_down):
    plane_count = lax.axis_size("ey")
    slot_count = EXPERTS * CAP
    tok_count = tokens.shape[0]
    model_width = tokens.shape[1]
    routes = expert_ids.reshape(-1)
    onehot = (routes[:, None] == jnp.arange(EXPERTS, dtype=jnp.int32)[None, :]).astype(jnp.int32)
    before = jnp.cumsum(onehot, axis=0) - onehot
    slot_place = jnp.sum(before * onehot, axis=1)
    target = routes * CAP + slot_place
    matches = (jnp.arange(slot_count, dtype=jnp.int32)[:, None] == target[None, :]).reshape(
        slot_count, tok_count, TOP
    )
    picker = jnp.any(matches, axis=2)
    slot_weight = jnp.sum(
        jnp.where(matches, route_weights[None, :, :], jnp.float32(0.0)), axis=(1, 2)
    )
    picker_low = picker.astype(jnp.bfloat16)
    sent_tokens = jnp.dot(picker_low, tokens, preferred_element_type=jnp.float32)
    sent_tokens = sent_tokens.astype(jnp.bfloat16).reshape(plane_count, CAP, model_width)
    sent_cot = jnp.dot(picker_low, cotangent, preferred_element_type=jnp.float32)
    sent_cot = (
        (sent_cot * slot_weight[:, None]).astype(jnp.bfloat16).reshape(plane_count, CAP, model_width)
    )
    member_count = lax.axis_size("ez")
    place = lax.axis_index("ez")
    block_width = w_gate.shape[0]
    stacked = jnp.stack([w_gate, w_up, w_down.T], axis=0)
    forward = [(i, (i + 1) % member_count) for i in range(member_count)]
    backward = [(i, (i - 1) % member_count) for i in range(member_count)]
    half_steps = member_count // 2
    cw = stacked
    ccw = stacked
    by_distance = [None] * member_count
    by_distance[0] = stacked
    for step in range(1, half_steps):
        cw = lax.ppermute(cw, "ez", forward)
        ccw = lax.ppermute(ccw, "ez", backward)
        by_distance[step] = cw
        by_distance[member_count - step] = ccw
    cut = block_width // 2
    far_low = lax.ppermute(cw[:, :cut], "ez", forward)
    far_high = lax.ppermute(ccw[:, cut:], "ez", backward)
    by_distance[half_steps] = jnp.concatenate([far_low, far_high], axis=1)
    origin = (place - jnp.arange(member_count, dtype=jnp.int32)) % member_count
    gate_full = jnp.concatenate([chunk[0] for chunk in by_distance], axis=0)
    up_full = jnp.concatenate([chunk[1] for chunk in by_distance], axis=0)
    down_full = jnp.concatenate([chunk[2] for chunk in by_distance], axis=0)
    member_tokens = lax.all_to_all(sent_tokens, "ey", split_axis=0, concat_axis=0, tiled=True)
    member_cot = lax.all_to_all(sent_cot, "ey", split_axis=0, concat_axis=0, tiled=True)
    row_total = plane_count * CAP
    member_tokens = jnp.take(
        member_tokens.reshape(row_total, member_count, block_width), origin, axis=1
    ).reshape(row_total, model_width)
    member_cot = jnp.take(
        member_cot.reshape(row_total, member_count, block_width), origin, axis=1
    ).reshape(row_total, model_width)
    gate_pre = jnp.dot(member_tokens, gate_full, preferred_element_type=jnp.float32)
    up_pre = jnp.dot(member_tokens, up_full, preferred_element_type=jnp.float32)
    hidden_grad = jnp.dot(member_cot, down_full, preferred_element_type=jnp.float32)
    hidden, gate_grad, up_grad = activate(gate_pre, up_pre, hidden_grad)
    out_part = lax.dot_general(
        hidden, down_full, (((1,), (1,)), ((), ())), preferred_element_type=jnp.float32
    )
    in_part = lax.dot_general(
        gate_grad, gate_full, (((1,), (1,)), ((), ())), preferred_element_type=jnp.float32
    )
    in_part = in_part + lax.dot_general(
        up_grad, up_full, (((1,), (1,)), ((), ())), preferred_element_type=jnp.float32
    )
    results = jnp.stack([out_part, in_part], axis=1).astype(jnp.bfloat16)
    results = results.reshape(row_total, 2, member_count, block_width)
    pair_count = lax.axis_size("tc")
    chip_count = lax.axis_size("tx")
    core = lax.axis_index("tc")
    out_width = model_width // (chip_count * pair_count)
    per_out = out_width // block_width
    base = (
        jnp.arange(chip_count, dtype=jnp.int32)[:, None] * (pair_count * per_out)
        + jnp.arange(per_out, dtype=jnp.int32)[None, :]
    ).reshape(-1)
    own = jnp.take(results, origin[base + core * per_out], axis=2)
    other = jnp.take(results, origin[base + (1 - core) * per_out], axis=2)
    other = lax.ppermute(other, "tc", [(0, 1), (1, 0)])
    pair_sum = (own.astype(jnp.float32) + other.astype(jnp.float32)).astype(jnp.bfloat16)
    pair_sum = pair_sum.reshape(row_total, 2, chip_count, out_width)
    summed = lax.psum_scatter(pair_sum, "tx", scatter_dimension=2, tiled=True)
    rounded = summed.reshape(plane_count, CAP, 2, -1)
    plane = lax.axis_index("ey")
    from_shift = [lax.dynamic_index_in_dim(rounded, plane, axis=0, keepdims=False)]
    for shift in range(1, plane_count):
        piece = lax.dynamic_index_in_dim(
            rounded, (plane + shift) % plane_count, axis=0, keepdims=False
        )
        pairs = [(i, (i + shift) % plane_count) for i in range(plane_count)]
        from_shift.append(lax.ppermute(piece, "ey", pairs))
    returned = jnp.take(
        jnp.stack(from_shift, axis=0),
        (plane - jnp.arange(plane_count, dtype=jnp.int32)) % plane_count,
        axis=0,
    )
    returned = returned.reshape(slot_count, 2, -1).astype(jnp.float32)
    picker_full = picker.astype(jnp.float32)
    weighted = picker_full * slot_weight[:, None]
    mixed = jnp.dot(weighted.T, returned[:, 0], precision=lax.Precision.HIGHEST).astype(
        jnp.bfloat16
    )
    grad_tokens = jnp.dot(picker_full.T, returned[:, 1], precision=lax.Precision.HIGHEST).astype(
        jnp.bfloat16
    )
    return (mixed, grad_tokens)


def solution(mesh):
    ed_size = mesh.shape["ed"]
    member_count = ed_size // EXPERTS
    pair_count = 2
    devices = np.asarray(mesh.devices).reshape(
        EXPERTS, member_count, mesh.shape["tp"] // pair_count, pair_count
    )
    split_mesh = Mesh(devices, ("ey", "ez", "tx", "tc"))
    ed = ("ey", "ez")
    tp = ("tx", "tc")
    return jax.shard_map(
        per_device,
        mesh=split_mesh,
        in_specs=(
            P(ed, None),
            P(ed, None),
            P(ed, None),
            P(ed, None),
            P(ed, tp),
            P(ed, tp),
            P(tp, ed),
        ),
        out_specs=(P(ed, tp), P(ed, tp)),
        check_vma=False,
    )
```

```python
import jax
import jax.numpy as jnp
import numpy as np
from jax import lax
from jax.sharding import Mesh
from jax.sharding import PartitionSpec as P

EXPERTS = 4
TOP = 2
CAP = 80


def activate(gate_pre, up_pre, hidden_grad):
    sig_gate = jax.nn.sigmoid(gate_pre)
    silu_gate = gate_pre * sig_gate
    hidden = (silu_gate * up_pre).astype(jnp.bfloat16)
    gate_grad = (hidden_grad * up_pre * sig_gate * (1.0 + gate_pre * (1.0 - sig_gate))).astype(
        jnp.bfloat16
    )
    up_grad = (hidden_grad * silu_gate).astype(jnp.bfloat16)
    return (hidden, gate_grad, up_grad)


def per_device(tokens, cotangent, expert_ids, route_weights, w_gate, w_up, w_down):
    plane_count = lax.axis_size("ey")
    slot_count = EXPERTS * CAP
    tok_count = tokens.shape[0]
    model_width = tokens.shape[1]
    routes = expert_ids.reshape(-1)
    onehot = (routes[:, None] == jnp.arange(EXPERTS, dtype=jnp.int32)[None, :]).astype(jnp.int32)
    before = jnp.cumsum(onehot, axis=0) - onehot
    slot_place = jnp.sum(before * onehot, axis=1)
    target = routes * CAP + slot_place
    matches = (jnp.arange(slot_count, dtype=jnp.int32)[:, None] == target[None, :]).reshape(
        slot_count, tok_count, TOP
    )
    picker = jnp.any(matches, axis=2)
    slot_weight = jnp.sum(
        jnp.where(matches, route_weights[None, :, :], jnp.float32(0.0)), axis=(1, 2)
    )
    picker_low = picker.astype(jnp.bfloat16)
    sent_tokens = jnp.dot(picker_low, tokens, preferred_element_type=jnp.float32)
    sent_tokens = sent_tokens.astype(jnp.bfloat16).reshape(plane_count, CAP, model_width)
    sent_cot = jnp.dot(picker_low, cotangent, preferred_element_type=jnp.float32)
    sent_cot = (
        (sent_cot * slot_weight[:, None]).astype(jnp.bfloat16).reshape(plane_count, CAP, model_width)
    )
    member_count = lax.axis_size("ez")
    place = lax.axis_index("ez")
    block_width = w_gate.shape[0]
    down_pieces = lax.all_gather(w_down, "ez", axis=0, tiled=False)
    stacked = jnp.stack([w_gate, w_up], axis=0)
    forward = [(i, (i + 1) % member_count) for i in range(member_count)]
    backward = [(i, (i - 1) % member_count) for i in range(member_count)]
    half_steps = member_count // 2
    cw = stacked
    ccw = stacked
    by_distance = [None] * member_count
    by_distance[0] = stacked
    for step in range(1, half_steps):
        cw = lax.ppermute(cw, "ez", forward)
        ccw = lax.ppermute(ccw, "ez", backward)
        by_distance[step] = cw
        by_distance[member_count - step] = ccw
    cut = block_width // 2
    far_low = lax.ppermute(cw[:, :cut], "ez", forward)
    far_high = lax.ppermute(ccw[:, cut:], "ez", backward)
    by_distance[half_steps] = jnp.concatenate([far_low, far_high], axis=1)
    origin = (place - jnp.arange(member_count, dtype=jnp.int32)) % member_count
    gate_full = jnp.concatenate([chunk[0] for chunk in by_distance], axis=0)
    up_full = jnp.concatenate([chunk[1] for chunk in by_distance], axis=0)
    member_tokens = lax.all_to_all(sent_tokens, "ey", split_axis=0, concat_axis=0, tiled=True)
    member_cot = lax.all_to_all(sent_cot, "ey", split_axis=0, concat_axis=0, tiled=True)
    row_total = plane_count * CAP
    member_tokens = jnp.take(
        member_tokens.reshape(row_total, member_count, block_width), origin, axis=1
    ).reshape(row_total, model_width)
    member_cot = member_cot.reshape(row_total, member_count, block_width)
    gate_pre = jnp.dot(member_tokens, gate_full, preferred_element_type=jnp.float32)
    up_pre = jnp.dot(member_tokens, up_full, preferred_element_type=jnp.float32)
    hidden_grad = lax.dot_general(
        member_cot, down_pieces, (((1, 2), (0, 2)), ((), ())), preferred_element_type=jnp.float32
    )
    hidden, gate_grad, up_grad = activate(gate_pre, up_pre, hidden_grad)
    out_part = lax.dot_general(
        hidden, down_pieces, (((1,), (1,)), ((), ())), preferred_element_type=jnp.float32
    )
    in_part = lax.dot_general(
        gate_grad, gate_full, (((1,), (1,)), ((), ())), preferred_element_type=jnp.float32
    )
    in_part = in_part + lax.dot_general(
        up_grad, up_full, (((1,), (1,)), ((), ())), preferred_element_type=jnp.float32
    )
    in_part = jnp.take(in_part.reshape(row_total, member_count, block_width), origin, axis=1)
    results = jnp.stack([out_part, in_part], axis=1).astype(jnp.bfloat16)
    results = results.reshape(row_total, 2, model_width)
    summed = lax.psum_scatter(results, "tp", scatter_dimension=2, tiled=True)
    rounded = summed.reshape(plane_count, CAP, 2, -1)
    returned = lax.all_to_all(rounded, "ey", split_axis=0, concat_axis=0, tiled=True)
    returned = returned.reshape(slot_count, 2, -1).astype(jnp.float32)
    picker_full = picker.astype(jnp.float32)
    weighted = picker_full * slot_weight[:, None]
    mixed = jnp.dot(weighted.T, returned[:, 0], precision=lax.Precision.HIGHEST).astype(
        jnp.bfloat16
    )
    grad_tokens = jnp.dot(picker_full.T, returned[:, 1], precision=lax.Precision.HIGHEST).astype(
        jnp.bfloat16
    )
    return (mixed, grad_tokens)


def solution(mesh):
    ed_size = mesh.shape["ed"]
    member_count = ed_size // EXPERTS
    devices = np.asarray(mesh.devices).reshape(EXPERTS, member_count, mesh.shape["tp"])
    split_mesh = Mesh(devices, ("ey", "ez", "tp"))
    ed = ("ey", "ez")
    return jax.shard_map(
        per_device,
        mesh=split_mesh,
        in_specs=(
            P(ed, None),
            P(ed, None),
            P(ed, None),
            P(ed, None),
            P(ed, "tp"),
            P(ed, "tp"),
            P("tp", ed),
        ),
        out_specs=(P(ed, "tp"), P(ed, "tp")),
        check_vma=False,
    )
```

```python
import jax
import jax.numpy as jnp
import numpy as np
from jax import lax
from jax.sharding import Mesh
from jax.sharding import PartitionSpec as P

EXPERTS = 4
TOP = 2
CAP = 80


def activate(gate_pre, up_pre, hidden_grad):
    sig_gate = jax.nn.sigmoid(gate_pre)
    silu_gate = gate_pre * sig_gate
    hidden = (silu_gate * up_pre).astype(jnp.bfloat16)
    gate_grad = (hidden_grad * up_pre * sig_gate * (1.0 + gate_pre * (1.0 - sig_gate))).astype(
        jnp.bfloat16
    )
    up_grad = (hidden_grad * silu_gate).astype(jnp.bfloat16)
    return (hidden, gate_grad, up_grad)


def per_device(tokens, cotangent, expert_ids, route_weights, w_gate, w_up, w_down):
    plane_count = lax.axis_size("ey")
    slot_count = EXPERTS * CAP
    tok_count = tokens.shape[0]
    model_width = tokens.shape[1]
    routes = expert_ids.reshape(-1)
    onehot = (routes[:, None] == jnp.arange(EXPERTS, dtype=jnp.int32)[None, :]).astype(jnp.int32)
    before = jnp.cumsum(onehot, axis=0) - onehot
    slot_place = jnp.sum(before * onehot, axis=1)
    target = routes * CAP + slot_place
    matches = (jnp.arange(slot_count, dtype=jnp.int32)[:, None] == target[None, :]).reshape(
        slot_count, tok_count, TOP
    )
    picker = jnp.any(matches, axis=2)
    slot_weight = jnp.sum(
        jnp.where(matches, route_weights[None, :, :], jnp.float32(0.0)), axis=(1, 2)
    )
    picker_low = picker.astype(jnp.bfloat16)
    sent_tokens = jnp.dot(picker_low, tokens, preferred_element_type=jnp.float32)
    sent_tokens = sent_tokens.astype(jnp.bfloat16).reshape(plane_count, CAP, model_width)
    sent_cot = jnp.dot(picker_low, cotangent, preferred_element_type=jnp.float32)
    sent_cot = (
        (sent_cot * slot_weight[:, None]).astype(jnp.bfloat16).reshape(plane_count, CAP, model_width)
    )
    member_count = lax.axis_size("ez")
    place = lax.axis_index("ez")
    block_width = w_gate.shape[0]
    stacked = jnp.stack([w_gate, w_up, w_down.T], axis=0)
    far = 4
    group = member_count // far

    def shifted(value, distance):
        pairs = [(i, (i + distance) % member_count) for i in range(member_count)]
        return lax.ppermute(value, "ez", pairs)

    cut = block_width // 2
    by_distance = [None] * member_count
    long_cw = shifted(stacked, far)
    long_ccw = shifted(stacked, -far)
    long_low = shifted(long_cw[:, :cut], far)
    long_high = shifted(long_ccw[:, cut:], -far)
    long_block = [stacked, long_cw, jnp.concatenate([long_low, long_high], axis=1), long_ccw]
    for m in range(group):
        by_distance[far * m] = long_block[m]
    long_block = jnp.stack(long_block, axis=0)
    near_cw = shifted(long_block, 1)
    near_ccw = shifted(long_block, -1)
    near_low = shifted(near_cw[:, :, :cut], 1)
    near_high = shifted(near_ccw[:, :, cut:], -1)
    for m in range(group):
        by_distance[1 + far * m] = near_cw[m]
        by_distance[(far * m - 1) % member_count] = near_ccw[m]
        by_distance[2 + far * m] = jnp.concatenate(
            [near_low[m], near_high[(m + 1) % group]], axis=1
        )
    origin = (place - jnp.arange(member_count, dtype=jnp.int32)) % member_count
    gate_full = jnp.concatenate([chunk[0] for chunk in by_distance], axis=0)
    up_full = jnp.concatenate([chunk[1] for chunk in by_distance], axis=0)
    down_full = jnp.concatenate([chunk[2] for chunk in by_distance], axis=0)
    member_tokens = lax.all_to_all(sent_tokens, "ey", split_axis=0, concat_axis=0, tiled=True)
    member_cot = lax.all_to_all(sent_cot, "ey", split_axis=0, concat_axis=0, tiled=True)
    row_total = plane_count * CAP
    member_tokens = jnp.take(
        member_tokens.reshape(row_total, member_count, block_width), origin, axis=1
    ).reshape(row_total, model_width)
    member_cot = jnp.take(
        member_cot.reshape(row_total, member_count, block_width), origin, axis=1
    ).reshape(row_total, model_width)
    gate_pre = jnp.dot(member_tokens, gate_full, preferred_element_type=jnp.float32)
    up_pre = jnp.dot(member_tokens, up_full, preferred_element_type=jnp.float32)
    hidden_grad = jnp.dot(member_cot, down_full, preferred_element_type=jnp.float32)
    hidden, gate_grad, up_grad = activate(gate_pre, up_pre, hidden_grad)
    out_part = lax.dot_general(
        hidden, down_full, (((1,), (1,)), ((), ())), preferred_element_type=jnp.float32
    )
    in_part = lax.dot_general(
        gate_grad, gate_full, (((1,), (1,)), ((), ())), preferred_element_type=jnp.float32
    )
    in_part = in_part + lax.dot_general(
        up_grad, up_full, (((1,), (1,)), ((), ())), preferred_element_type=jnp.float32
    )
    results = jnp.stack([out_part, in_part], axis=1).astype(jnp.bfloat16)
    results = jnp.take(
        results.reshape(row_total, 2, member_count, block_width), origin, axis=2
    ).reshape(row_total, 2, model_width)
    summed = lax.psum_scatter(results, "tp", scatter_dimension=2, tiled=True)
    rounded = summed.reshape(plane_count, CAP, 2, -1)
    returned = lax.all_to_all(rounded, "ey", split_axis=0, concat_axis=0, tiled=True)
    returned = returned.reshape(slot_count, 2, -1).astype(jnp.float32)
    picker_full = picker.astype(jnp.float32)
    weighted = picker_full * slot_weight[:, None]
    mixed = jnp.dot(weighted.T, returned[:, 0], precision=lax.Precision.HIGHEST).astype(
        jnp.bfloat16
    )
    grad_tokens = jnp.dot(picker_full.T, returned[:, 1], precision=lax.Precision.HIGHEST).astype(
        jnp.bfloat16
    )
    return (mixed, grad_tokens)


def solution(mesh):
    ed_size = mesh.shape["ed"]
    member_count = ed_size // EXPERTS
    devices = np.asarray(mesh.devices).reshape(EXPERTS, member_count, mesh.shape["tp"])
    split_mesh = Mesh(devices, ("ey", "ez", "tp"))
    ed = ("ey", "ez")
    return jax.shard_map(
        per_device,
        mesh=split_mesh,
        in_specs=(
            P(ed, None),
            P(ed, None),
            P(ed, None),
            P(ed, None),
            P(ed, "tp"),
            P(ed, "tp"),
            P("tp", ed),
        ),
        out_specs=(P(ed, "tp"), P(ed, "tp")),
        check_vma=False,
    )
```

```python
import jax
import jax.numpy as jnp
import numpy as np
from jax import lax
from jax.sharding import Mesh
from jax.sharding import PartitionSpec as P

EXPERTS = 4
TOP = 2
CAP = 80


def activate(gate_pre, up_pre, hidden_grad):
    sig_gate = jax.nn.sigmoid(gate_pre)
    silu_gate = gate_pre * sig_gate
    hidden = (silu_gate * up_pre).astype(jnp.bfloat16)
    gate_grad = (hidden_grad * up_pre * sig_gate * (1.0 + gate_pre * (1.0 - sig_gate))).astype(
        jnp.bfloat16
    )
    up_grad = (hidden_grad * silu_gate).astype(jnp.bfloat16)
    return (hidden, gate_grad, up_grad)


def per_device(tokens, cotangent, expert_ids, route_weights, w_gate, w_up, w_down):
    plane_count = lax.axis_size("ey")
    slot_count = EXPERTS * CAP
    tok_count = tokens.shape[0]
    model_width = tokens.shape[1]
    routes = expert_ids.reshape(-1)
    onehot = (routes[:, None] == jnp.arange(EXPERTS, dtype=jnp.int32)[None, :]).astype(jnp.int32)
    before = jnp.cumsum(onehot, axis=0) - onehot
    slot_place = jnp.sum(before * onehot, axis=1)
    target = routes * CAP + slot_place
    matches = (jnp.arange(slot_count, dtype=jnp.int32)[:, None] == target[None, :]).reshape(
        slot_count, tok_count, TOP
    )
    picker = jnp.any(matches, axis=2)
    slot_weight = jnp.sum(
        jnp.where(matches, route_weights[None, :, :], jnp.float32(0.0)), axis=(1, 2)
    )
    picker_low = picker.astype(jnp.bfloat16)
    sent_tokens = jnp.dot(picker_low, tokens, preferred_element_type=jnp.float32)
    sent_tokens = sent_tokens.astype(jnp.bfloat16).reshape(plane_count, CAP, model_width)
    sent_cot = jnp.dot(picker_low, cotangent, preferred_element_type=jnp.float32)
    sent_cot = (
        (sent_cot * slot_weight[:, None]).astype(jnp.bfloat16).reshape(plane_count, CAP, model_width)
    )
    member_count = lax.axis_size("ez")
    place = lax.axis_index("ez")
    block_width = w_gate.shape[0]
    stacked = jnp.stack([w_gate, w_up, w_down.T], axis=0)
    forward = [(i, (i + 1) % member_count) for i in range(member_count)]
    backward = [(i, (i - 1) % member_count) for i in range(member_count)]
    half_steps = member_count // 2
    cw = stacked
    ccw = stacked
    by_distance = [None] * member_count
    by_distance[0] = stacked
    for step in range(1, half_steps):
        cw = lax.ppermute(cw, "ez", forward)
        ccw = lax.ppermute(ccw, "ez", backward)
        by_distance[step] = cw
        by_distance[member_count - step] = ccw
    cut = block_width // 2
    far_low = lax.ppermute(cw[:, :cut], "ez", forward)
    far_high = lax.ppermute(ccw[:, cut:], "ez", backward)
    by_distance[half_steps] = jnp.concatenate([far_low, far_high], axis=1)
    origin = (place - jnp.arange(member_count, dtype=jnp.int32)) % member_count
    gate_full = jnp.concatenate([chunk[0] for chunk in by_distance], axis=0)
    up_full = jnp.concatenate([chunk[1] for chunk in by_distance], axis=0)
    down_full = jnp.concatenate([chunk[2] for chunk in by_distance], axis=0)
    member_tokens = lax.all_to_all(sent_tokens, "ey", split_axis=0, concat_axis=0, tiled=True)
    member_cot = lax.all_to_all(sent_cot, "ey", split_axis=0, concat_axis=0, tiled=True)
    row_total = plane_count * CAP
    member_tokens = jnp.take(
        member_tokens.reshape(row_total, member_count, block_width), origin, axis=1
    ).reshape(row_total, model_width)
    member_cot = jnp.take(
        member_cot.reshape(row_total, member_count, block_width), origin, axis=1
    ).reshape(row_total, model_width)
    gate_pre = jnp.dot(member_tokens, gate_full, preferred_element_type=jnp.float32)
    up_pre = jnp.dot(member_tokens, up_full, preferred_element_type=jnp.float32)
    hidden_grad = jnp.dot(member_cot, down_full, preferred_element_type=jnp.float32)
    hidden, gate_grad, up_grad = activate(gate_pre, up_pre, hidden_grad)
    halves = 2
    part_slots = CAP // halves

    def slot_half(value, half):
        value = value.reshape(plane_count, CAP, -1)[:, half * part_slots : (half + 1) * part_slots]
        return value.reshape(plane_count * part_slots, -1)

    returned_parts = []
    for half in range(halves):
        hidden_h = slot_half(hidden, half)
        gate_grad_h = slot_half(gate_grad, half)
        up_grad_h = slot_half(up_grad, half)
        out_part = lax.dot_general(
            hidden_h, down_full, (((1,), (1,)), ((), ())), preferred_element_type=jnp.float32
        )
        in_part = lax.dot_general(
            gate_grad_h, gate_full, (((1,), (1,)), ((), ())), preferred_element_type=jnp.float32
        )
        in_part = in_part + lax.dot_general(
            up_grad_h, up_full, (((1,), (1,)), ((), ())), preferred_element_type=jnp.float32
        )
        part_rows = plane_count * part_slots
        results = jnp.stack([out_part, in_part], axis=1).astype(jnp.bfloat16)
        results = jnp.take(
            results.reshape(part_rows, 2, member_count, block_width), origin, axis=2
        ).reshape(part_rows, 2, model_width)
        summed = lax.psum_scatter(results, "tp", scatter_dimension=2, tiled=True)
        rounded = summed.reshape(plane_count, part_slots, 2, -1)
        returned_parts.append(
            lax.all_to_all(rounded, "ey", split_axis=0, concat_axis=0, tiled=True)
        )
    returned = jnp.concatenate(returned_parts, axis=1)
    returned = returned.reshape(slot_count, 2, -1).astype(jnp.float32)
    picker_full = picker.astype(jnp.float32)
    weighted = picker_full * slot_weight[:, None]
    mixed = jnp.dot(weighted.T, returned[:, 0], precision=lax.Precision.HIGHEST).astype(
        jnp.bfloat16
    )
    grad_tokens = jnp.dot(picker_full.T, returned[:, 1], precision=lax.Precision.HIGHEST).astype(
        jnp.bfloat16
    )
    return (mixed, grad_tokens)


def solution(mesh):
    ed_size = mesh.shape["ed"]
    member_count = ed_size // EXPERTS
    devices = np.asarray(mesh.devices).reshape(EXPERTS, member_count, mesh.shape["tp"])
    split_mesh = Mesh(devices, ("ey", "ez", "tp"))
    ed = ("ey", "ez")
    return jax.shard_map(
        per_device,
        mesh=split_mesh,
        in_specs=(
            P(ed, None),
            P(ed, None),
            P(ed, None),
            P(ed, None),
            P(ed, "tp"),
            P(ed, "tp"),
            P("tp", ed),
        ),
        out_specs=(P(ed, "tp"), P(ed, "tp")),
        check_vma=False,
    )
```

```python
import jax
import jax.numpy as jnp
import numpy as np
from jax import lax
from jax.sharding import Mesh
from jax.sharding import PartitionSpec as P

EXPERTS = 4
TOP = 2
CAP = 80


def activate(gate_pre, up_pre, hidden_grad):
    sig_gate = jax.nn.sigmoid(gate_pre)
    silu_gate = gate_pre * sig_gate
    hidden = (silu_gate * up_pre).astype(jnp.bfloat16)
    gate_grad = (hidden_grad * up_pre * sig_gate * (1.0 + gate_pre * (1.0 - sig_gate))).astype(
        jnp.bfloat16
    )
    up_grad = (hidden_grad * silu_gate).astype(jnp.bfloat16)
    return (hidden, gate_grad, up_grad)


def per_device(tokens, cotangent, expert_ids, route_weights, w_gate, w_up, w_down):
    plane_count = lax.axis_size("ey")
    slot_count = EXPERTS * CAP
    tok_count = tokens.shape[0]
    model_width = tokens.shape[1]
    routes = expert_ids.reshape(-1)
    onehot = (routes[:, None] == jnp.arange(EXPERTS, dtype=jnp.int32)[None, :]).astype(jnp.int32)
    before = jnp.cumsum(onehot, axis=0) - onehot
    slot_place = jnp.sum(before * onehot, axis=1)
    target = routes * CAP + slot_place
    matches = (jnp.arange(slot_count, dtype=jnp.int32)[:, None] == target[None, :]).reshape(
        slot_count, tok_count, TOP
    )
    picker = jnp.any(matches, axis=2)
    slot_weight = jnp.sum(
        jnp.where(matches, route_weights[None, :, :], jnp.float32(0.0)), axis=(1, 2)
    )
    picker_low = picker.astype(jnp.bfloat16)
    sent_tokens = jnp.dot(picker_low, tokens, preferred_element_type=jnp.float32)
    sent_tokens = sent_tokens.astype(jnp.bfloat16).reshape(plane_count, CAP, model_width)
    sent_cot = jnp.dot(picker_low, cotangent, preferred_element_type=jnp.float32)
    sent_cot = (
        (sent_cot * slot_weight[:, None]).astype(jnp.bfloat16).reshape(plane_count, CAP, model_width)
    )
    member_count = lax.axis_size("ez")
    place = lax.axis_index("ez")
    block_width = w_gate.shape[0]
    stacked = jnp.stack([w_gate, w_up, w_down.T], axis=0)
    forward = [(i, (i + 1) % member_count) for i in range(member_count)]
    backward = [(i, (i - 1) % member_count) for i in range(member_count)]
    half_steps = member_count // 2
    cw = stacked
    ccw = stacked
    by_distance = [None] * member_count
    by_distance[0] = stacked
    for step in range(1, half_steps):
        cw = lax.ppermute(cw, "ez", forward)
        ccw = lax.ppermute(ccw, "ez", backward)
        by_distance[step] = cw
        by_distance[member_count - step] = ccw
    cut = block_width // 2
    far_low = lax.ppermute(cw[:, :cut], "ez", forward)
    far_high = lax.ppermute(ccw[:, cut:], "ez", backward)
    by_distance[half_steps] = jnp.concatenate([far_low, far_high], axis=1)
    origin = (place - jnp.arange(member_count, dtype=jnp.int32)) % member_count
    gate_full = jnp.concatenate([chunk[0] for chunk in by_distance], axis=0)
    up_full = jnp.concatenate([chunk[1] for chunk in by_distance], axis=0)
    down_full = jnp.concatenate([chunk[2] for chunk in by_distance], axis=0)
    member_tokens = lax.all_to_all(sent_tokens, "ey", split_axis=0, concat_axis=0, tiled=True)
    member_cot = lax.all_to_all(sent_cot, "ey", split_axis=0, concat_axis=0, tiled=True)
    row_total = plane_count * CAP
    member_tokens = jnp.take(
        member_tokens.reshape(row_total, member_count, block_width), origin, axis=1
    ).reshape(row_total, model_width)
    member_cot = jnp.take(
        member_cot.reshape(row_total, member_count, block_width), origin, axis=1
    ).reshape(row_total, model_width)
    gate_pre = jnp.dot(member_tokens, gate_full, preferred_element_type=jnp.float32)
    up_pre = jnp.dot(member_tokens, up_full, preferred_element_type=jnp.float32)
    hidden_grad = jnp.dot(member_cot, down_full, preferred_element_type=jnp.float32)
    hidden, gate_grad, up_grad = activate(gate_pre, up_pre, hidden_grad)
    out_part = lax.dot_general(
        hidden, down_full, (((1,), (1,)), ((), ())), preferred_element_type=jnp.float32
    )
    in_part = lax.dot_general(
        gate_grad, gate_full, (((1,), (1,)), ((), ())), preferred_element_type=jnp.float32
    )
    in_part = in_part + lax.dot_general(
        up_grad, up_full, (((1,), (1,)), ((), ())), preferred_element_type=jnp.float32
    )
    results = jnp.stack([out_part, in_part], axis=1).astype(jnp.bfloat16)
    results = jnp.take(
        results.reshape(row_total, 2, member_count, block_width), origin, axis=2
    ).reshape(row_total, 2, model_width)
    tp_count = lax.axis_size("tp")
    pieces = results.reshape(row_total, 2, tp_count, model_width // tp_count)
    pieces = lax.all_to_all(pieces, "tp", split_axis=2, concat_axis=2, tiled=True)
    summed = jnp.sum(pieces.astype(jnp.float32), axis=2).astype(jnp.bfloat16)
    rounded = summed.reshape(plane_count, CAP, 2, -1)
    returned = lax.all_to_all(rounded, "ey", split_axis=0, concat_axis=0, tiled=True)
    returned = returned.reshape(slot_count, 2, -1).astype(jnp.float32)
    picker_full = picker.astype(jnp.float32)
    weighted = picker_full * slot_weight[:, None]
    mixed = jnp.dot(weighted.T, returned[:, 0], precision=lax.Precision.HIGHEST).astype(
        jnp.bfloat16
    )
    grad_tokens = jnp.dot(picker_full.T, returned[:, 1], precision=lax.Precision.HIGHEST).astype(
        jnp.bfloat16
    )
    return (mixed, grad_tokens)


def solution(mesh):
    ed_size = mesh.shape["ed"]
    member_count = ed_size // EXPERTS
    devices = np.asarray(mesh.devices).reshape(EXPERTS, member_count, mesh.shape["tp"])
    split_mesh = Mesh(devices, ("ey", "ez", "tp"))
    ed = ("ey", "ez")
    return jax.shard_map(
        per_device,
        mesh=split_mesh,
        in_specs=(
            P(ed, None),
            P(ed, None),
            P(ed, None),
            P(ed, None),
            P(ed, "tp"),
            P(ed, "tp"),
            P("tp", ed),
        ),
        out_specs=(P(ed, "tp"), P(ed, "tp")),
        check_vma=False,
    )
```

```python
import jax
import jax.numpy as jnp
import numpy as np
from jax import lax
from jax.sharding import Mesh
from jax.sharding import PartitionSpec as P

EXPERTS = 4
TOP = 2
CAP = 80


def activate(gate_pre, up_pre, hidden_grad):
    sig_gate = jax.nn.sigmoid(gate_pre)
    silu_gate = gate_pre * sig_gate
    hidden = (silu_gate * up_pre).astype(jnp.bfloat16)
    gate_grad = (hidden_grad * up_pre * sig_gate * (1.0 + gate_pre * (1.0 - sig_gate))).astype(
        jnp.bfloat16
    )
    up_grad = (hidden_grad * silu_gate).astype(jnp.bfloat16)
    return (hidden, gate_grad, up_grad)


def per_device(tokens, cotangent, expert_ids, route_weights, w_gate, w_up, w_down):
    plane_count = lax.axis_size("ey")
    slot_count = EXPERTS * CAP
    tok_count = tokens.shape[0]
    model_width = tokens.shape[1]
    routes = expert_ids.reshape(-1)
    onehot = (routes[:, None] == jnp.arange(EXPERTS, dtype=jnp.int32)[None, :]).astype(jnp.int32)
    before = jnp.cumsum(onehot, axis=0) - onehot
    slot_place = jnp.sum(before * onehot, axis=1)
    target = routes * CAP + slot_place
    matches = (jnp.arange(slot_count, dtype=jnp.int32)[:, None] == target[None, :]).reshape(
        slot_count, tok_count, TOP
    )
    picker = jnp.any(matches, axis=2)
    slot_weight = jnp.sum(
        jnp.where(matches, route_weights[None, :, :], jnp.float32(0.0)), axis=(1, 2)
    )
    picker_low = picker.astype(jnp.bfloat16)
    sent_tokens = jnp.dot(picker_low, tokens, preferred_element_type=jnp.float32)
    sent_tokens = sent_tokens.astype(jnp.bfloat16).reshape(plane_count, CAP, model_width)
    sent_cot = jnp.dot(picker_low, cotangent, preferred_element_type=jnp.float32)
    sent_cot = (
        (sent_cot * slot_weight[:, None]).astype(jnp.bfloat16).reshape(plane_count, CAP, model_width)
    )
    member_count = lax.axis_size("ez")
    place = lax.axis_index("ez")
    block_width = w_gate.shape[0]
    stacked = jnp.stack([w_gate, w_up, w_down.T], axis=0)
    forward = [(i, (i + 1) % member_count) for i in range(member_count)]
    backward = [(i, (i - 1) % member_count) for i in range(member_count)]
    half_steps = member_count // 2
    cw = stacked
    ccw = stacked
    by_distance = [None] * member_count
    by_distance[0] = stacked
    for step in range(1, half_steps):
        cw = lax.ppermute(cw, "ez", forward)
        ccw = lax.ppermute(ccw, "ez", backward)
        by_distance[step] = cw
        by_distance[member_count - step] = ccw
    cut = block_width // 2
    far_low = lax.ppermute(cw[:, :cut], "ez", forward)
    far_high = lax.ppermute(ccw[:, cut:], "ez", backward)
    by_distance[half_steps] = jnp.concatenate([far_low, far_high], axis=1)
    origin = (place - jnp.arange(member_count, dtype=jnp.int32)) % member_count
    gate_full = jnp.concatenate([chunk[0] for chunk in by_distance], axis=0)
    up_full = jnp.concatenate([chunk[1] for chunk in by_distance], axis=0)
    down_full = jnp.concatenate([chunk[2] for chunk in by_distance], axis=0)
    member_tokens = lax.all_to_all(sent_tokens, "ey", split_axis=0, concat_axis=0, tiled=True)
    member_cot = lax.all_to_all(sent_cot, "ey", split_axis=0, concat_axis=0, tiled=True)
    row_total = plane_count * CAP
    member_tokens = jnp.take(
        member_tokens.reshape(row_total, member_count, block_width), origin, axis=1
    ).reshape(row_total, model_width)
    member_cot = jnp.take(
        member_cot.reshape(row_total, member_count, block_width), origin, axis=1
    ).reshape(row_total, model_width)
    gate_pre = jnp.dot(member_tokens, gate_full, preferred_element_type=jnp.float32)
    up_pre = jnp.dot(member_tokens, up_full, preferred_element_type=jnp.float32)
    hidden_grad = jnp.dot(member_cot, down_full, preferred_element_type=jnp.float32)
    hidden, gate_grad, up_grad = activate(gate_pre, up_pre, hidden_grad)
    out_part = lax.dot_general(
        hidden, down_full, (((1,), (1,)), ((), ())), preferred_element_type=jnp.float32
    )
    in_part = lax.dot_general(
        gate_grad, gate_full, (((1,), (1,)), ((), ())), preferred_element_type=jnp.float32
    )
    in_part = in_part + lax.dot_general(
        up_grad, up_full, (((1,), (1,)), ((), ())), preferred_element_type=jnp.float32
    )
    results = jnp.stack([out_part, in_part], axis=1).astype(jnp.bfloat16)
    results = jnp.take(
        results.reshape(row_total, 2, member_count, block_width), origin, axis=2
    ).reshape(row_total, 2, model_width)
    tp_count = lax.axis_size("tp")
    pieces = results.reshape(row_total, 2, tp_count, model_width // tp_count)
    pieces = jnp.transpose(pieces, (2, 0, 1, 3))
    pieces = lax.all_to_all(pieces, "tp", split_axis=0, concat_axis=0, tiled=True)
    summed = jnp.sum(pieces.astype(jnp.float32), axis=0).astype(jnp.bfloat16)
    rounded = summed.reshape(plane_count, CAP, 2, -1)
    returned = lax.all_to_all(rounded, "ey", split_axis=0, concat_axis=0, tiled=True)
    returned = returned.reshape(slot_count, 2, -1).astype(jnp.float32)
    picker_full = picker.astype(jnp.float32)
    weighted = picker_full * slot_weight[:, None]
    mixed = jnp.dot(weighted.T, returned[:, 0], precision=lax.Precision.HIGHEST).astype(
        jnp.bfloat16
    )
    grad_tokens = jnp.dot(picker_full.T, returned[:, 1], precision=lax.Precision.HIGHEST).astype(
        jnp.bfloat16
    )
    return (mixed, grad_tokens)


def solution(mesh):
    ed_size = mesh.shape["ed"]
    member_count = ed_size // EXPERTS
    devices = np.asarray(mesh.devices).reshape(EXPERTS, member_count, mesh.shape["tp"])
    split_mesh = Mesh(devices, ("ey", "ez", "tp"))
    ed = ("ey", "ez")
    return jax.shard_map(
        per_device,
        mesh=split_mesh,
        in_specs=(
            P(ed, None),
            P(ed, None),
            P(ed, None),
            P(ed, None),
            P(ed, "tp"),
            P(ed, "tp"),
            P("tp", ed),
        ),
        out_specs=(P(ed, "tp"), P(ed, "tp")),
        check_vma=False,
    )
```

```python
import jax
import jax.numpy as jnp
import numpy as np
from jax import lax
from jax.sharding import Mesh
from jax.sharding import PartitionSpec as P

EXPERTS = 4
TOP = 2
CAP = 80


def activate(gate_pre, up_pre, hidden_grad):
    sig_gate = jax.nn.sigmoid(gate_pre)
    silu_gate = gate_pre * sig_gate
    hidden = (silu_gate * up_pre).astype(jnp.bfloat16)
    gate_grad = (hidden_grad * up_pre * sig_gate * (1.0 + gate_pre * (1.0 - sig_gate))).astype(
        jnp.bfloat16
    )
    up_grad = (hidden_grad * silu_gate).astype(jnp.bfloat16)
    return (hidden, gate_grad, up_grad)


def per_device(tokens, cotangent, expert_ids, route_weights, w_gate, w_up, w_down):
    plane_count = lax.axis_size("ey")
    slot_count = EXPERTS * CAP
    tok_count = tokens.shape[0]
    model_width = tokens.shape[1]
    routes = expert_ids.reshape(-1)
    onehot = (routes[:, None] == jnp.arange(EXPERTS, dtype=jnp.int32)[None, :]).astype(jnp.int32)
    before = jnp.cumsum(onehot, axis=0) - onehot
    slot_place = jnp.sum(before * onehot, axis=1)
    target = routes * CAP + slot_place
    matches = (jnp.arange(slot_count, dtype=jnp.int32)[:, None] == target[None, :]).reshape(
        slot_count, tok_count, TOP
    )
    picker = jnp.any(matches, axis=2)
    slot_weight = jnp.sum(
        jnp.where(matches, route_weights[None, :, :], jnp.float32(0.0)), axis=(1, 2)
    )
    picker_low = picker.astype(jnp.bfloat16)
    sent_tokens = jnp.dot(picker_low, tokens, preferred_element_type=jnp.float32)
    sent_tokens = sent_tokens.astype(jnp.bfloat16).reshape(plane_count, CAP, model_width)
    sent_cot = jnp.dot(picker_low, cotangent, preferred_element_type=jnp.float32)
    sent_cot = (
        (sent_cot * slot_weight[:, None]).astype(jnp.bfloat16).reshape(plane_count, CAP, model_width)
    )
    member_count = lax.axis_size("ez")
    place = lax.axis_index("ez")
    block_width = w_gate.shape[0]
    stacked = jnp.stack([w_gate, w_up, w_down.T], axis=0)
    forward = [(i, (i + 1) % member_count) for i in range(member_count)]
    backward = [(i, (i - 1) % member_count) for i in range(member_count)]
    half_steps = member_count // 2
    cw = stacked
    ccw = stacked
    by_distance = [None] * member_count
    by_distance[0] = stacked
    for step in range(1, half_steps):
        cw = lax.ppermute(cw, "ez", forward)
        ccw = lax.ppermute(ccw, "ez", backward)
        by_distance[step] = cw
        by_distance[member_count - step] = ccw
    cut = block_width // 2
    far_low = lax.ppermute(cw[:, :cut], "ez", forward)
    far_high = lax.ppermute(ccw[:, cut:], "ez", backward)
    by_distance[half_steps] = jnp.concatenate([far_low, far_high], axis=1)
    origin = (place - jnp.arange(member_count, dtype=jnp.int32)) % member_count
    gate_full = jnp.concatenate([chunk[0] for chunk in by_distance], axis=0)
    up_full = jnp.concatenate([chunk[1] for chunk in by_distance], axis=0)
    down_full = jnp.concatenate([chunk[2] for chunk in by_distance], axis=0)
    member_tokens = lax.all_to_all(sent_tokens, "ey", split_axis=0, concat_axis=0, tiled=True)
    member_cot = lax.all_to_all(sent_cot, "ey", split_axis=0, concat_axis=0, tiled=True)
    row_total = plane_count * CAP
    member_tokens = jnp.take(
        member_tokens.reshape(row_total, member_count, block_width), origin, axis=1
    ).reshape(row_total, model_width)
    member_cot = jnp.take(
        member_cot.reshape(row_total, member_count, block_width), origin, axis=1
    ).reshape(row_total, model_width)
    gate_pre = jnp.dot(member_tokens, gate_full, preferred_element_type=jnp.float32)
    up_pre = jnp.dot(member_tokens, up_full, preferred_element_type=jnp.float32)
    hidden_grad = jnp.dot(member_cot, down_full, preferred_element_type=jnp.float32)
    hidden, gate_grad, up_grad = activate(gate_pre, up_pre, hidden_grad)
    out_part = lax.dot_general(
        hidden, down_full, (((1,), (1,)), ((), ())), preferred_element_type=jnp.float32
    )
    in_part = lax.dot_general(
        gate_grad, gate_full, (((1,), (1,)), ((), ())), preferred_element_type=jnp.float32
    )
    in_part = in_part + lax.dot_general(
        up_grad, up_full, (((1,), (1,)), ((), ())), preferred_element_type=jnp.float32
    )
    results = jnp.stack([out_part, in_part], axis=1).astype(jnp.bfloat16)
    results = jnp.take(
        results.reshape(row_total, 2, member_count, block_width), origin, axis=2
    ).reshape(row_total, 2, model_width)
    tp_count = lax.axis_size("tp")
    pieces = results.reshape(plane_count, CAP, 2, tp_count, model_width // tp_count)
    pieces = jnp.transpose(pieces, (0, 3, 1, 2, 4)).reshape(plane_count * tp_count, CAP, 2, -1)
    pieces = lax.all_to_all(pieces, ("ey", "tp"), split_axis=0, concat_axis=0, tiled=True)
    pieces = pieces.reshape(plane_count, tp_count, CAP, 2, -1).astype(jnp.float32)
    returned = jnp.sum(pieces, axis=1).astype(jnp.bfloat16)
    returned = returned.reshape(slot_count, 2, -1).astype(jnp.float32)
    picker_full = picker.astype(jnp.float32)
    weighted = picker_full * slot_weight[:, None]
    mixed = jnp.dot(weighted.T, returned[:, 0], precision=lax.Precision.HIGHEST).astype(
        jnp.bfloat16
    )
    grad_tokens = jnp.dot(picker_full.T, returned[:, 1], precision=lax.Precision.HIGHEST).astype(
        jnp.bfloat16
    )
    return (mixed, grad_tokens)


def solution(mesh):
    ed_size = mesh.shape["ed"]
    member_count = ed_size // EXPERTS
    devices = np.asarray(mesh.devices).reshape(EXPERTS, member_count, mesh.shape["tp"])
    split_mesh = Mesh(devices, ("ey", "ez", "tp"))
    ed = ("ey", "ez")
    return jax.shard_map(
        per_device,
        mesh=split_mesh,
        in_specs=(
            P(ed, None),
            P(ed, None),
            P(ed, None),
            P(ed, None),
            P(ed, "tp"),
            P(ed, "tp"),
            P("tp", ed),
        ),
        out_specs=(P(ed, "tp"), P(ed, "tp")),
        check_vma=False,
    )
```

```python
import jax
import jax.numpy as jnp
import numpy as np
from jax import lax
from jax.sharding import Mesh
from jax.sharding import PartitionSpec as P

EXPERTS = 4
TOP = 2
CAP = 80


def activate(gate_pre, up_pre, hidden_grad):
    sig_gate = jax.nn.sigmoid(gate_pre)
    silu_gate = gate_pre * sig_gate
    hidden = (silu_gate * up_pre).astype(jnp.bfloat16)
    gate_grad = (hidden_grad * up_pre * sig_gate * (1.0 + gate_pre * (1.0 - sig_gate))).astype(
        jnp.bfloat16
    )
    up_grad = (hidden_grad * silu_gate).astype(jnp.bfloat16)
    return (hidden, gate_grad, up_grad)


def per_device(tokens, cotangent, expert_ids, route_weights, w_gate, w_up, w_down):
    plane_count = lax.axis_size("ey")
    slot_count = EXPERTS * CAP
    tok_count = tokens.shape[0]
    model_width = tokens.shape[1]
    routes = expert_ids.reshape(-1)
    onehot = (routes[:, None] == jnp.arange(EXPERTS, dtype=jnp.int32)[None, :]).astype(jnp.int32)
    before = jnp.cumsum(onehot, axis=0) - onehot
    slot_place = jnp.sum(before * onehot, axis=1)
    target = routes * CAP + slot_place
    matches = (jnp.arange(slot_count, dtype=jnp.int32)[:, None] == target[None, :]).reshape(
        slot_count, tok_count, TOP
    )
    picker = jnp.any(matches, axis=2)
    slot_weight = jnp.sum(
        jnp.where(matches, route_weights[None, :, :], jnp.float32(0.0)), axis=(1, 2)
    )
    picker_low = picker.astype(jnp.bfloat16)
    sent_tokens = jnp.dot(picker_low, tokens, preferred_element_type=jnp.float32)
    sent_tokens = sent_tokens.astype(jnp.bfloat16).reshape(plane_count, CAP, model_width)
    sent_cot = jnp.dot(picker_low, cotangent, preferred_element_type=jnp.float32)
    sent_cot = (
        (sent_cot * slot_weight[:, None]).astype(jnp.bfloat16).reshape(plane_count, CAP, model_width)
    )
    member_count = lax.axis_size("ez")
    place = lax.axis_index("ez")
    block_width = w_gate.shape[0]
    stacked = jnp.stack([w_gate, w_up, w_down.T], axis=0)
    forward = [(i, (i + 1) % member_count) for i in range(member_count)]
    backward = [(i, (i - 1) % member_count) for i in range(member_count)]
    half_steps = member_count // 2
    cw = stacked
    ccw = stacked
    by_distance = [None] * member_count
    by_distance[0] = stacked
    for step in range(1, half_steps):
        cw = lax.ppermute(cw, "ez", forward)
        ccw = lax.ppermute(ccw, "ez", backward)
        by_distance[step] = cw
        by_distance[member_count - step] = ccw
    cut = block_width // 2
    far_low = lax.ppermute(cw[:, :cut], "ez", forward)
    far_high = lax.ppermute(ccw[:, cut:], "ez", backward)
    by_distance[half_steps] = jnp.concatenate([far_low, far_high], axis=1)
    origin = (place - jnp.arange(member_count, dtype=jnp.int32)) % member_count
    gate_full = jnp.concatenate([chunk[0] for chunk in by_distance], axis=0)
    up_full = jnp.concatenate([chunk[1] for chunk in by_distance], axis=0)
    down_full = jnp.concatenate([chunk[2] for chunk in by_distance], axis=0)
    member_both = lax.all_to_all(
        jnp.stack([sent_tokens, sent_cot], axis=1), "ey", split_axis=0, concat_axis=0, tiled=True
    )
    member_tokens, member_cot = member_both[:, 0], member_both[:, 1]
    row_total = plane_count * CAP
    member_tokens = jnp.take(
        member_tokens.reshape(row_total, member_count, block_width), origin, axis=1
    ).reshape(row_total, model_width)
    member_cot = jnp.take(
        member_cot.reshape(row_total, member_count, block_width), origin, axis=1
    ).reshape(row_total, model_width)
    gate_pre = jnp.dot(member_tokens, gate_full, preferred_element_type=jnp.float32)
    up_pre = jnp.dot(member_tokens, up_full, preferred_element_type=jnp.float32)
    hidden_grad = jnp.dot(member_cot, down_full, preferred_element_type=jnp.float32)
    hidden, gate_grad, up_grad = activate(gate_pre, up_pre, hidden_grad)
    out_part = lax.dot_general(
        hidden, down_full, (((1,), (1,)), ((), ())), preferred_element_type=jnp.float32
    )
    in_part = lax.dot_general(
        gate_grad, gate_full, (((1,), (1,)), ((), ())), preferred_element_type=jnp.float32
    )
    in_part = in_part + lax.dot_general(
        up_grad, up_full, (((1,), (1,)), ((), ())), preferred_element_type=jnp.float32
    )
    results = jnp.stack([out_part, in_part], axis=1).astype(jnp.bfloat16)
    results = jnp.take(
        results.reshape(row_total, 2, member_count, block_width), origin, axis=2
    ).reshape(row_total, 2, model_width)
    tp_count = lax.axis_size("tp")
    pieces = results.reshape(plane_count, CAP, 2, tp_count, model_width // tp_count)
    pieces = jnp.transpose(pieces, (0, 3, 1, 2, 4)).reshape(plane_count * tp_count, CAP, 2, -1)
    pieces = lax.all_to_all(pieces, ("ey", "tp"), split_axis=0, concat_axis=0, tiled=True)
    pieces = pieces.reshape(plane_count, tp_count, CAP, 2, -1).astype(jnp.float32)
    returned = jnp.sum(pieces, axis=1).astype(jnp.bfloat16)
    returned = returned.reshape(slot_count, 2, -1).astype(jnp.float32)
    picker_full = picker.astype(jnp.float32)
    weighted = picker_full * slot_weight[:, None]
    mixed = jnp.dot(weighted.T, returned[:, 0], precision=lax.Precision.HIGHEST).astype(
        jnp.bfloat16
    )
    grad_tokens = jnp.dot(picker_full.T, returned[:, 1], precision=lax.Precision.HIGHEST).astype(
        jnp.bfloat16
    )
    return (mixed, grad_tokens)


def solution(mesh):
    ed_size = mesh.shape["ed"]
    member_count = ed_size // EXPERTS
    devices = np.asarray(mesh.devices).reshape(EXPERTS, member_count, mesh.shape["tp"])
    split_mesh = Mesh(devices, ("ey", "ez", "tp"))
    ed = ("ey", "ez")
    return jax.shard_map(
        per_device,
        mesh=split_mesh,
        in_specs=(
            P(ed, None),
            P(ed, None),
            P(ed, None),
            P(ed, None),
            P(ed, "tp"),
            P(ed, "tp"),
            P("tp", ed),
        ),
        out_specs=(P(ed, "tp"), P(ed, "tp")),
        check_vma=False,
    )
```
